32 devices in a mesh: rep: 16 (over z, y, x), tp: 2 (over core).
Axes of the slice: x: 2, y: 2, z: 4, core: 2. Of those that a mesh axis runs over, the one named last changes fastest.
Arguments:
- grads_narrow: bfloat16 [16, 1, 2, 1024, 512], P('rep', None, None, None, 'tp'), may hold values from -6 to 6
- errors_narrow: float32 [16, 1, 2, 1024, 512], P('rep', None, None, None, 'tp'), may hold values from -6 to 6
- starts_narrow: float32 [1, 2, 512, 32], P(None, None, 'tp'), may hold values from -6 to 6
- moment_narrow: float32 [1, 2, 524288], P(None, None, ('rep', 'tp')), may hold values from -0.75 to 0.75
- grads_square: bfloat16 [16, 1, 3, 1024, 1024], P('rep', None, None, None, 'tp'), may hold values from -6 to 6
- errors_square: float32 [16, 1, 3, 1024, 1024], P('rep', None, None, None, 'tp'), may hold values from -6 to 6
- starts_square: float32 [1, 3, 1024, 32], P(None, None, 'tp'), may hold values from -6 to 6
- moment_square: float32 [1, 3, 1048576], P(None, None, ('rep', 'tp')), may hold values from -0.75 to 0.75
Outputs:
- residue_narrow: float32 [16, 1, 2, 1024, 512], P('rep', None, None, None, 'tp')
- factor_narrow: float32 [1, 2, 512, 32], P(None, None, 'tp')
- velocity_narrow: float32 [1, 2, 524288], P(None, None, ('rep', 'tp'))
- residue_square: float32 [16, 1, 3, 1024, 1024], P('rep', None, None, None, 'tp')
- factor_square: float32 [1, 3, 1024, 32], P(None, None, 'tp')
- velocity_square: float32 [1, 3, 1048576], P(None, None, ('rep', 'tp'))
The draws below stay inside these ranges and needn't reach their ends.
All inputs are finite; a program needn't handle non-finite values.
Results may differ from the reference program's by a relative error of at most 0.0003.
Values sent between devices are 32-bit elements; how exact they have to be, the bound alone decides.
A program may use at most 128 MiB of HBM per device.

```python
import jax
import jax.numpy as jnp
from jax import lax

D = 1024
DK = 512
R = 32
ROUNDS = 2
NS_STEPS = 5
LAYERS = 1
REPLICAS = 16
N_REP = 16


def raised(drawn, own_key, source, target, parts, factor):
    def block_of(dim):
        return (jnp.arange(drawn.shape[dim]) // (drawn.shape[dim] // parts)).reshape((-1,) + (1,) * (drawn.ndim - 1 - dim))

    one_side = jax.random.permutation(own_key, parts)[block_of(target)]
    other_side = (block_of(target) + parts // 2) % parts
    return jnp.where((block_of(source) == one_side) | (block_of(source) == other_side), factor * drawn, drawn)


def shard_levels(stream_key, extent, shards, low, top_value):
    gain, own = 1.0, jax.random.fold_in(stream_key, 6)
    for position, shards_of in shards:
        draws = jnp.exp(jax.random.uniform(jax.random.fold_in(own, position), (shards_of,), jnp.float32, low / len(shards), top_value / len(shards)))
        gain = gain * jnp.repeat(draws, extent[position] // shards_of).reshape([-1 if axis == position else 1 for axis in range(len(extent))])
    return gain


def normal_values(rng, shape, spread, reach, pieces=(), dtype=jnp.bfloat16):
    gain = shard_levels(rng, shape, pieces, -0.22, 0.18) if pieces else 1.0
    drawn = jax.random.normal(rng, shape, jnp.float32) * spread * gain
    return jnp.minimum(jnp.maximum(drawn, -reach), reach).astype(dtype)


def heavy_noise(rng, dims, scale, bound, pieces, heavy, kind=jnp.bfloat16):
    drawn = scale * jax.random.normal(rng, dims, jnp.float32)
    if pieces:
        drawn = drawn * shard_levels(rng, dims, pieces, -0.22, 0.18)
    return jnp.clip(raised(drawn, jax.random.fold_in(rng, 3), *heavy), -bound, bound).astype(kind)


def setup_inputs(seed: int = 0) -> dict:
    key_list = jax.random.split(jax.random.key(seed), 9)
    grads_narrow = heavy_noise(key_list[0], (REPLICAS, LAYERS, 2, D, DK), 1.0, 6.0, ((0, 16), (4, 2)), (0, 3, 16, 2.0))
    errors_narrow = normal_values(key_list[1], (REPLICAS, LAYERS, 2, D, DK), 0.5, 6.0, ((0, 16), (4, 2)), jnp.float32)
    starts_narrow = normal_values(key_list[2], (LAYERS, 2, DK, R), 1.0, 6.0, ((2, 2),), jnp.float32)
    moment_narrow = normal_values(key_list[3], (LAYERS, 2, D * DK), 0.05, 0.75, ((2, 32),), jnp.float32)
    grads_square = heavy_noise(key_list[4], (REPLICAS, LAYERS, 3, D, D), 1.0, 6.0, ((0, 16), (4, 2)), (0, 3, 16, 2.0))
    errors_square = normal_values(key_list[5], (REPLICAS, LAYERS, 3, D, D), 0.5, 6.0, ((0, 16), (4, 2)), jnp.float32)
    starts_square = normal_values(key_list[6], (LAYERS, 3, D, R), 1.0, 6.0, ((2, 2),), jnp.float32)
    moment_square = normal_values(key_list[7], (LAYERS, 3, D * D), 0.05, 0.75, ((2, 32),), jnp.float32)
    return dict(grads_narrow=grads_narrow, errors_narrow=errors_narrow, starts_narrow=starts_narrow, moment_narrow=moment_narrow, grads_square=grads_square, errors_square=errors_square, starts_square=starts_square, moment_square=moment_square)


epsilon = 1e-06
momentum_decay = 0.9
highest = lax.Precision.HIGHEST

def orthonormal(panel):
    scaled = panel / (jnp.sqrt(jnp.sum(panel * panel)) + epsilon)
    for sweep in range(NS_STEPS):
        gram = lax.dot_general(scaled, scaled, (((0,), (0,)), ((), ())), precision=highest)
        scaled = 1.5 * scaled - 0.5 * jnp.dot(scaled, gram, precision=highest)
    return scaled

def compress(grads, errors, start, moment):
    merged = grads.astype(jnp.float32) + errors
    factor = start
    ortho = None
    for turn in range(ROUNDS):
        panel = jnp.einsum('rdn,nk->dk', merged, factor, precision=highest)
        ortho = orthonormal(panel)
        factor = jnp.einsum('rdn,dk->nk', merged, ortho, precision=highest) / N_REP
    approx = lax.dot_general(ortho, factor, (((1,), (1,)), ((), ())), precision=highest)
    residue = merged - approx[None]
    velocity = momentum_decay * moment + approx.reshape(-1)
    return (residue, factor, velocity)

def group(grads, errors, starts, moment, count):
    residues, factors, velocities = ([], [], [])
    for layer in range(LAYERS):
        res_layer, fac_layer, vel_layer = ([], [], [])
        for which in range(count):
            res, fac, vel = compress(grads[:, layer, which], errors[:, layer, which], starts[layer, which], moment[layer, which])
            res_layer.append(res)
            fac_layer.append(fac)
            vel_layer.append(vel)
        residues.append(jnp.stack(res_layer, axis=1))
        factors.append(jnp.stack(fac_layer, axis=0))
        velocities.append(jnp.stack(vel_layer, axis=0))
    return (jnp.stack(residues, axis=1), jnp.stack(factors, axis=0), jnp.stack(velocities, axis=0))

def reference(grads_narrow, errors_narrow, starts_narrow, moment_narrow, grads_square, errors_square, starts_square, moment_square):
    res_n, fac_n, vel_n = group(grads_narrow, errors_narrow, starts_narrow, moment_narrow, 2)
    res_s, fac_s, vel_s = group(grads_square, errors_square, starts_square, moment_square, 3)
    return (res_n, fac_n, vel_n, res_s, fac_s, vel_s)
```

```python
import functools

import jax
import jax.numpy as jnp
from jax import lax
from jax.experimental import pallas as pl
from jax.experimental.pallas import tpu as pltpu
from jax.sharding import PartitionSpec as P

ROUNDS = 2
NS_STEPS = 5
LANES = 128
BAND = 256
VMEM_LIMIT = 48 * 1024 * 1024

epsilon = 1e-06
momentum_decay = 0.9
highest = lax.Precision.HIGHEST
f32, bf16 = jnp.float32, jnp.bfloat16
MESH = pl.DeviceIdType.MESH


def split(x):
    hi = x.astype(bf16)
    lo = (x - hi.astype(f32)).astype(bf16)
    return hi, lo


def dot(a, b, dims, precision=None):
    return lax.dot_general(a, b, (dims, ((), ())), precision=precision, preferred_element_type=f32)


NN, NT, TN = ((1,), (0,)), ((1,), (1,)), ((0,), (0,))


def first_blocks(widths):
    first, at = [], 0
    for width in widths:
        first.append(at)
        at += width // LANES
    return first, at


def factor_of(ref, first, width, rank, offset=0):
    pieces = [
        ref[(offset + first + b) * rank : (offset + first + b + 1) * rank, :]
        for b in range(width // LANES)
    ]
    return jnp.concatenate(pieces, axis=1)


def left_band(out_ref, item, rank, stacked, hi, lo):
    both = dot(stacked, hi, NT)
    band = both[:rank] + both[rank:] + dot(stacked[:rank], lo, NT)
    for b in range(BAND // LANES):
        out_ref[b, item * rank : (item + 1) * rank, :] = band[:, b * LANES : (b + 1) * LANES]


def first_left_kernel(rank, gn, en, gs, es, sn, ss, panel, hn, ln, hs, ls, fn, fs):
    @pl.when(pl.program_id(0) == 0)
    def _():
        for start, keep in ((sn, fn), (ss, fs)):
            for which in range(start.shape[0]):
                keep[which] = jnp.concatenate(split(start[which].T), axis=0)

    item = 0
    for g, e, h, l, keep in ((gn, en, hn, ln, fn), (gs, es, hs, ls, fs)):
        for which in range(g.shape[0]):
            hi, lo = split(g[which].astype(f32) + e[which])
            h[which], l[which] = hi, lo
            left_band(panel, item, rank, keep[which], hi, lo)
            item += 1


def left_kernel(rank, replicas, factor, hn, ln, hs, ls, panel, fn, fs):
    counts = (hn.shape[0], hs.shape[0])
    widths = [hn.shape[2]] * counts[0] + [hs.shape[2]] * counts[1]
    first, _ = first_blocks(widths)

    @pl.when(pl.program_id(0) == 0)
    def _():
        item = 0
        for keep in (fn, fs):
            for which in range(keep.shape[0]):
                whole = factor_of(factor, first[item], widths[item], rank) / replicas
                keep[which] = jnp.concatenate(split(whole), axis=0)
                item += 1

    item = 0
    for h, l, keep in ((hn, ln, fn), (hs, ls, fs)):
        for which in range(h.shape[0]):
            left_band(panel, item, rank, keep[which], h[which], l[which])
            item += 1


def right_kernel(rank, items, panel, hn, ln, hs, ls, ortho, factor):
    step = pl.program_id(0)
    blocks = panel.shape[0]
    size = items * rank

    @pl.when(step == 0)
    def _():
        stacked = jnp.concatenate([panel[b] for b in range(blocks)], axis=1)
        scaled = []
        for item in range(items):
            part = stacked[item * rank : (item + 1) * rank]
            scaled.append(part / (jnp.sqrt(jnp.sum(part * part)) + epsilon))
        scaled = jnp.concatenate(scaled, axis=0)
        row = lax.broadcasted_iota(jnp.int32, (size, size), 0)
        column = lax.broadcasted_iota(jnp.int32, (size, size), 1)
        own = (row // rank) == (column // rank)
        identity = jnp.where(row == column, 1.0, 0.0).astype(f32)
        gram = jnp.where(own, dot(scaled, scaled, NT, highest), 0.0)
        total = None
        for sweep in range(NS_STEPS):
            turn = 1.5 * identity - 0.5 * gram
            total = turn if total is None else dot(turn, total, NN, highest)
            if sweep < NS_STEPS - 1:
                gram = dot(dot(turn, gram, NN, highest), turn, NN, highest)
        result = dot(total, scaled, NN, highest)
        for b in range(blocks):
            ortho[b] = result[:, b * LANES : (b + 1) * LANES]
        factor[...] = jnp.zeros_like(factor)

    per = BAND // LANES
    band = jnp.concatenate([ortho[step * per + b] for b in range(per)], axis=1)
    item = at = 0
    for h, l in ((hn, ln), (hs, ls)):
        for which in range(h.shape[0]):
            hi, lo = split(band[item * rank : (item + 1) * rank])
            both = dot(jnp.concatenate([hi, lo], axis=0), h[which], NN)
            term = both[:rank] + both[rank:] + dot(hi, l[which], NN)
            for b in range(h.shape[2] // LANES):
                factor[at : at + rank, :] += term[:, b * LANES : (b + 1) * LANES]
                at += rank
            item += 1


def last_kernel(
    rank, replicas, ortho, both, hn, ln, hs, ls, mn, ms,
    rn, rs, fn, fs, vn, vs, kn, ks, rows_n, rows_s,
):
    step = pl.program_id(0)
    counts = (hn.shape[0], hs.shape[0])
    widths = [hn.shape[2]] * counts[0] + [hs.shape[2]] * counts[1]
    first, blocks = first_blocks(widths)
    tp = lax.axis_index("tp")
    place = lax.axis_index("rep") * lax.axis_size("tp") + tp
    own = pl.multiple_of(tp * blocks * rank, blocks * rank)

    def wide(whole):
        hi, lo = split(whole)
        return jnp.concatenate([hi, hi, lo], axis=0)

    def tall(part):
        hi, lo = split(part)
        return jnp.concatenate([hi, lo, hi], axis=0)

    @pl.when(step == 0)
    def _():
        item = 0
        for f, k, m, v, rows_ref in ((fn, kn, mn, vn, rows_n), (fs, ks, ms, vs, rows_s)):
            rows = m.shape[1]
            at = place * rows
            block, inside = at // LANES, lax.rem(at, LANES)
            for which in range(f.shape[0]):
                width = widths[item]
                pieces = [
                    both[pl.ds(own + (first[item] + b) * rank, rank), :]
                    for b in range(width // LANES)
                ]
                mine = jnp.concatenate(pieces, axis=1) / replicas
                f[which] = mine.T
                k[which] = wide(mine)
                full = jnp.concatenate(
                    [factor_of(both, first[item], width, rank, core * blocks) for core in range(2)],
                    axis=1,
                )
                left = tall(ortho[block, item * rank : (item + 1) * rank, :])
                rows_ref[...] = dot(left, wide(full / replicas), TN)
                v[which] = momentum_decay * m[which] + rows_ref[
                    pl.ds(pl.multiple_of(inside, 8), rows), :
                ]
                item += 1

    per = BAND // LANES
    band = jnp.concatenate([ortho[step * per + b] for b in range(per)], axis=1)
    item = 0
    for h, l, k, r in ((hn, ln, kn, rn), (hs, ls, ks, rs)):
        for which in range(h.shape[0]):
            left = tall(band[item * rank : (item + 1) * rank])
            approx = dot(left, k[which], TN)
            r[which] = (h[which].astype(f32) + l[which].astype(f32)) - approx
            item += 1


NEAR = 4


def sum_kernel(replicas, over_tp, gather_tp, x, out, acc, in_tp, in_near, in_far, sems_s, sems_r):
    near = NEAR
    far = replicas // near
    rep, tp = lax.axis_index("rep"), lax.axis_index("tp")
    a, b = lax.rem(rep, near), rep // near
    other = {"tp": 1 - tp, "rep": rep}

    def near_id(j):
        return {"rep": b * near + lax.rem(a + j, near), "tp": tp}

    def far_id(j):
        return {"rep": lax.rem(b + j, far) * near + a, "tp": tp}

    barrier = pltpu.get_barrier_semaphore()
    partners = [near_id(j) for j in range(1, near)] + [far_id(j) for j in range(1, far)]
    if over_tp or gather_tp:
        partners.append(other)
    for partner in partners:
        pl.semaphore_signal(barrier, inc=1, device_id=partner, device_id_type=MESH)
    pl.semaphore_wait(barrier, len(partners))

    counter = [0]

    def send(src, dst, device):
        i = counter[0]
        counter[0] += 1
        copy = pltpu.make_async_remote_copy(
            src_ref=src, dst_ref=dst, send_sem=sems_s.at[i], recv_sem=sems_r.at[i],
            device_id=device, device_id_type=MESH,
        )
        copy.start()
        return copy

    def finish(copies):
        for copy in copies:
            copy.wait()

    def ds(at, size):
        return pl.ds(pl.multiple_of(at, 8), size)

    rows = x.shape[0]
    part = rows // 2 if over_tp else rows
    quarter = part // near
    slice_ = quarter // far

    if over_tp:
        base = tp * part
        finish([send(x.at[ds((1 - tp) * part, part)], in_tp, other)])
        acc[ds(base, part), :] = x[ds(base, part), :] + in_tp[...]
        src = acc
    else:
        base = tp * 0
        src = x

    finish([
        send(src.at[ds(base + lax.rem(a + j, near) * quarter, quarter)], in_near.at[j - 1], near_id(j))
        for j in range(1, near)
    ])
    mine = base + a * quarter
    value = src[ds(mine, quarter), :]
    for j in range(1, near):
        value = value + in_near[j - 1]
    acc[ds(mine, quarter), :] = value

    finish([
        send(acc.at[ds(mine + lax.rem(b + j, far) * slice_, slice_)], in_far.at[j - 1], far_id(j))
        for j in range(1, far)
    ])
    leaf = mine + b * slice_
    value = acc[ds(leaf, slice_), :]
    for j in range(1, far):
        value = value + in_far[j - 1]
    shift = tp * rows if gather_tp else 0
    out[ds(shift + leaf, slice_), :] = value

    def spread(at, size, ids):
        at = shift + at
        finish([send(out.at[ds(at, size)], out.at[ds(at, size)], device) for device in ids])

    spread(leaf, slice_, [far_id(j) for j in range(1, far)])
    spread(mine, quarter, [near_id(j) for j in range(1, near)])
    if over_tp:
        spread(base, part, [other])
    if gather_tp:
        spread(0, rows, [other])


def all_sum(x, replicas, over_tp, gather_tp, collective_id):
    rows = x.shape[0]
    far = replicas // NEAR
    part = rows // 2 if over_tp else rows
    quarter = part // NEAR
    copies = 2 * (NEAR - 1 + far - 1 + 1)
    return pl.pallas_call(
        functools.partial(sum_kernel, replicas, over_tp, gather_tp),
        out_shape=jax.ShapeDtypeStruct((rows * (2 if gather_tp else 1), LANES), f32),
        in_specs=[pl.BlockSpec(memory_space=pltpu.VMEM)],
        out_specs=pl.BlockSpec(memory_space=pltpu.VMEM),
        scratch_shapes=[
            pltpu.VMEM((rows, LANES), f32),
            pltpu.VMEM((part, LANES), f32),
            pltpu.VMEM((NEAR - 1, quarter, LANES), f32),
            pltpu.VMEM((far - 1, quarter // far, LANES), f32),
            pltpu.SemaphoreType.DMA((copies,)),
            pltpu.SemaphoreType.DMA((copies,)),
        ],
        compiler_params=pltpu.CompilerParams(
            collective_id=collective_id, has_side_effects=True, vmem_limit_bytes=VMEM_LIMIT
        ),
        name=f"all_sum_{collective_id}",
    )(x)


def padded_sum(x, replicas, over_tp, gather_tp, collective_id):
    rows = x.shape[0]
    unit = 8 * replicas * (2 if over_tp else 1)
    extra = -rows % unit
    if extra:
        x = jnp.pad(x, ((0, extra), (0, 0)))
    total = all_sum(x, replicas, over_tp, gather_tp, collective_id)
    if extra:
        if gather_tp:
            total = total.reshape(2, rows + extra, LANES)[:, :rows].reshape(2 * rows, LANES)
        else:
            total = total[:rows]
    return total


def on_device(gn, en, sn, mn, gs, es, ss, ms):
    replicas = lax.axis_size("rep")
    shape_gn, shape_gs, shape_sn, shape_ss = gn.shape, gs.shape, sn.shape, ss.shape
    shape_mn, shape_ms = mn.shape, ms.shape
    gn, en, gs, es = (
        x.reshape((x.shape[1] * x.shape[2],) + x.shape[3:]) for x in (gn, en, gs, es)
    )
    sn, ss = (x.reshape((-1,) + x.shape[2:]) for x in (sn, ss))
    cn, depth, wn = gn.shape
    cs, _, ws = gs.shape
    rank = sn.shape[-1]
    items = cn + cs
    steps, per, blocks = depth // BAND, BAND // LANES, depth // LANES
    factor_rows = (cn * wn + cs * ws) // LANES * rank
    mn = mn.reshape(cn, -1, 2 * wn)
    ms = ms.reshape(cs, -1, 2 * ws)

    band_n = pl.BlockSpec((cn, BAND, wn), lambda t: (0, t, 0))
    band_s = pl.BlockSpec((cs, BAND, ws), lambda t: (0, t, 0))
    bands = [band_n, band_n, band_s, band_s]

    def full(shape):
        return pl.BlockSpec(shape, lambda t: (0,) * len(shape))

    panel_band = pl.BlockSpec((per, items * rank, LANES), lambda t: (t, 0, 0))
    panel_shape = jax.ShapeDtypeStruct((blocks, items * rank, LANES), f32)
    keep = [pltpu.VMEM((cn, 2 * rank, wn), bf16), pltpu.VMEM((cs, 2 * rank, ws), bf16)]
    params = pltpu.CompilerParams(vmem_limit_bytes=VMEM_LIMIT)

    panel, hn, ln, hs, ls = pl.pallas_call(
        functools.partial(first_left_kernel, rank),
        grid=(steps,),
        in_specs=bands + [full(sn.shape), full(ss.shape)],
        out_specs=[panel_band] + bands,
        out_shape=[
            panel_shape,
            jax.ShapeDtypeStruct(gn.shape, bf16),
            jax.ShapeDtypeStruct(gn.shape, bf16),
            jax.ShapeDtypeStruct(gs.shape, bf16),
            jax.ShapeDtypeStruct(gs.shape, bf16),
        ],
        scratch_shapes=keep,
        compiler_params=params,
        name="first_left",
    )(gn, en, gs, es, sn, ss)

    for turn in range(ROUNDS):
        if turn:
            panel = pl.pallas_call(
                functools.partial(left_kernel, rank, replicas),
                grid=(steps,),
                in_specs=[full(factor.shape)] + bands,
                out_specs=panel_band,
                out_shape=panel_shape,
                scratch_shapes=keep,
                compiler_params=params,
                name="left",
            )(factor, hn, ln, hs, ls)
        panel = padded_sum(panel.reshape(-1, LANES), replicas, True, False, 0)
        panel = panel.reshape(panel_shape.shape)
        ortho, factor = pl.pallas_call(
            functools.partial(right_kernel, rank, items),
            grid=(steps,),
            in_specs=[full(panel_shape.shape)] + bands,
            out_specs=[full(panel_shape.shape), full((factor_rows, LANES))],
            out_shape=[panel_shape, jax.ShapeDtypeStruct((factor_rows, LANES), f32)],
            compiler_params=params,
            name="right",
        )(panel, hn, ln, hs, ls)
        final = turn == ROUNDS - 1
        factor = padded_sum(factor, replicas, False, final, 2 if final else 1)

    rn, rs, fn, fs, vn, vs = pl.pallas_call(
        functools.partial(last_kernel, rank, replicas),
        grid=(steps,),
        in_specs=[full(panel_shape.shape), full(factor.shape)]
        + bands
        + [full(mn.shape), full(ms.shape)],
        out_specs=[
            band_n, band_s, full(sn.shape), full(ss.shape), full(mn.shape), full(ms.shape),
        ],
        out_shape=[
            jax.ShapeDtypeStruct(x.shape, f32) for x in (gn, gs, sn, ss, mn, ms)
        ],
        scratch_shapes=[
            pltpu.VMEM((cn, 3 * rank, wn), bf16),
            pltpu.VMEM((cs, 3 * rank, ws), bf16),
            pltpu.VMEM((LANES, 2 * wn), f32),
            pltpu.VMEM((LANES, 2 * ws), f32),
        ],
        compiler_params=params,
        name="last",
    )(ortho, factor, hn, ln, hs, ls, mn, ms)
    return (
        rn.reshape(shape_gn),
        fn.reshape(shape_sn),
        vn.reshape(shape_mn),
        rs.reshape(shape_gs),
        fs.reshape(shape_ss),
        vs.reshape(shape_ms),
    )


def solution(mesh):
    in_specs = (
        P("rep", None, None, None, "tp"),
        P("rep", None, None, None, "tp"),
        P(None, None, "tp", None),
        P(None, None, ("rep", "tp")),
        P("rep", None, None, None, "tp"),
        P("rep", None, None, None, "tp"),
        P(None, None, "tp", None),
        P(None, None, ("rep", "tp")),
    )
    out_specs = (
        P("rep", None, None, None, "tp"),
        P(None, None, "tp", None),
        P(None, None, ("rep", "tp")),
        P("rep", None, None, None, "tp"),
        P(None, None, "tp", None),
        P(None, None, ("rep", "tp")),
    )
    return jax.shard_map(
        on_device, mesh=mesh, in_specs=in_specs, out_specs=out_specs, check_vma=False
    )
```

```python
import functools

import jax
import jax.numpy as jnp
from jax import lax
from jax.experimental import pallas as pl
from jax.experimental.pallas import tpu as pltpu
from jax.sharding import PartitionSpec as P

ROUNDS = 2
NS_STEPS = 5
LANES = 128
BAND = 256
VMEM_LIMIT = 24 * 1024 * 1024

epsilon = 1e-06
momentum_decay = 0.9
highest = lax.Precision.HIGHEST
f32, bf16 = jnp.float32, jnp.bfloat16
MESH = pl.DeviceIdType.MESH


def split(x):
    hi = x.astype(bf16)
    lo = (x - hi.astype(f32)).astype(bf16)
    return hi, lo


def dot(a, b, dims, precision=None):
    return lax.dot_general(a, b, (dims, ((), ())), precision=precision, preferred_element_type=f32)


NN, NT, TN = ((1,), (0,)), ((1,), (1,)), ((0,), (0,))


def first_blocks(widths):
    first, at = [], 0
    for width in widths:
        first.append(at)
        at += width // LANES
    return first, at


def factor_of(ref, first, width, rank, offset=0):
    pieces = [
        ref[(offset + first + b) * rank : (offset + first + b + 1) * rank, :]
        for b in range(width // LANES)
    ]
    return jnp.concatenate(pieces, axis=1)


def left_band(out_ref, item, rank, stacked, hi, lo):
    both = dot(stacked, hi, NT)
    band = both[:rank] + both[rank:] + dot(stacked[:rank], lo, NT)
    for b in range(BAND // LANES):
        out_ref[b, item * rank : (item + 1) * rank, :] = band[:, b * LANES : (b + 1) * LANES]


def first_left_kernel(rank, gn, en, gs, es, sn, ss, panel, hn, ln, hs, ls, fn, fs):
    @pl.when(pl.program_id(0) == 0)
    def _():
        for start, keep in ((sn, fn), (ss, fs)):
            for which in range(start.shape[0]):
                keep[which] = jnp.concatenate(split(start[which]), axis=0)

    item = 0
    for g, e, h, l, keep in ((gn, en, hn, ln, fn), (gs, es, hs, ls, fs)):
        for which in range(g.shape[0]):
            hi, lo = split(g[which].astype(f32) + e[which])
            h[which], l[which] = hi, lo
            left_band(panel, item, rank, keep[which], hi, lo)
            item += 1


def left_kernel(rank, replicas, factor, hn, ln, hs, ls, panel, fn, fs):
    counts = (hn.shape[0], hs.shape[0])
    widths = [hn.shape[2]] * counts[0] + [hs.shape[2]] * counts[1]
    first, _ = first_blocks(widths)

    @pl.when(pl.program_id(0) == 0)
    def _():
        item = 0
        for keep in (fn, fs):
            for which in range(keep.shape[0]):
                whole = factor_of(factor, first[item], widths[item], rank) / replicas
                keep[which] = jnp.concatenate(split(whole), axis=0)
                item += 1

    item = 0
    for h, l, keep in ((hn, ln, fn), (hs, ls, fs)):
        for which in range(h.shape[0]):
            left_band(panel, item, rank, keep[which], h[which], l[which])
            item += 1


def right_kernel(rank, items, panel, hn, ln, hs, ls, ortho, factor):
    step = pl.program_id(0)
    blocks = panel.shape[0]
    size = items * rank

    @pl.when(step == 0)
    def _():
        stacked = jnp.concatenate([panel[b] for b in range(blocks)], axis=1)
        scaled = []
        for item in range(items):
            part = stacked[item * rank : (item + 1) * rank]
            scaled.append(part / (jnp.sqrt(jnp.sum(part * part)) + epsilon))
        scaled = jnp.concatenate(scaled, axis=0)
        row = lax.broadcasted_iota(jnp.int32, (size, size), 0)
        column = lax.broadcasted_iota(jnp.int32, (size, size), 1)
        own = (row // rank) == (column // rank)
        identity = jnp.where(row == column, 1.0, 0.0).astype(f32)
        gram = jnp.where(own, dot(scaled, scaled, NT, highest), 0.0)
        total = None
        for sweep in range(NS_STEPS):
            turn = 1.5 * identity - 0.5 * gram
            total = turn if total is None else dot(turn, total, NN, highest)
            if sweep < NS_STEPS - 1:
                gram = dot(dot(turn, gram, NN, highest), turn, NN, highest)
        result = dot(total, scaled, NN, highest)
        for b in range(blocks):
            ortho[b] = result[:, b * LANES : (b + 1) * LANES]
        factor[...] = jnp.zeros_like(factor)

    per = BAND // LANES
    band = jnp.concatenate([ortho[step * per + b] for b in range(per)], axis=1)
    item = at = 0
    for h, l in ((hn, ln), (hs, ls)):
        for which in range(h.shape[0]):
            hi, lo = split(band[item * rank : (item + 1) * rank])
            both = dot(jnp.concatenate([hi, lo], axis=0), h[which], NN)
            term = both[:rank] + both[rank:] + dot(hi, l[which], NN)
            for b in range(h.shape[2] // LANES):
                factor[at : at + rank, :] += term[:, b * LANES : (b + 1) * LANES]
                at += rank
            item += 1


def last_kernel(
    rank, replicas, ortho, both, hn, ln, hs, ls, mn, ms,
    rn, rs, fn, fs, vn, vs, kn, ks, rows_n, rows_s,
):
    step = pl.program_id(0)
    counts = (hn.shape[0], hs.shape[0])
    widths = [hn.shape[2]] * counts[0] + [hs.shape[2]] * counts[1]
    first, blocks = first_blocks(widths)
    tp = lax.axis_index("tp")
    place = lax.axis_index("rep") * lax.axis_size("tp") + tp
    own = pl.multiple_of(tp * blocks * rank, blocks * rank)

    def wide(whole):
        hi, lo = split(whole)
        return jnp.concatenate([hi, hi, lo], axis=0)

    def tall(part):
        hi, lo = split(part)
        return jnp.concatenate([hi, lo, hi], axis=0)

    @pl.when(step == 0)
    def _():
        item = 0
        for f, k, m, v, rows_ref in ((fn, kn, mn, vn, rows_n), (fs, ks, ms, vs, rows_s)):
            per_row = rows_ref.shape[0]
            rows = m.shape[0] // (f.shape[0] * per_row)
            interleaved = f is fn
            at = place * rows
            block, inside = at // LANES, lax.rem(at, LANES)
            for which in range(f.shape[0]):
                width = widths[item]
                pieces = [
                    both[pl.ds(own + (first[item] + b) * rank, rank), :]
                    for b in range(width // LANES)
                ]
                mine = jnp.concatenate(pieces, axis=1) / replicas
                f[which] = mine
                k[which] = wide(mine)
                full = jnp.concatenate(
                    [factor_of(both, first[item], width, rank, core * blocks) for core in range(2)],
                    axis=1,
                )
                left = tall(ortho[block, item * rank : (item + 1) * rank, :])
                approx = dot(left, wide(full / replicas), TN)
                for c in range(per_row):
                    rows_ref[c] = approx[:, c * LANES : (c + 1) * LANES]
                for c in range(per_row):
                    if interleaved:
                        spot = pl.ds(c * f.shape[0] + which, rows, stride=per_row * f.shape[0])
                    else:
                        spot = pl.ds(which * rows * per_row + c, rows, stride=per_row)
                    v[spot, :] = (
                        momentum_decay * m[spot, :]
                        + rows_ref[c, pl.ds(pl.multiple_of(inside, 8), rows), :]
                    )
                item += 1

    per = BAND // LANES
    band = jnp.concatenate([ortho[step * per + b] for b in range(per)], axis=1)
    item = 0
    for h, l, k, r in ((hn, ln, kn, rn), (hs, ls, ks, rs)):
        for which in range(h.shape[0]):
            left = tall(band[item * rank : (item + 1) * rank])
            approx = dot(left, k[which], TN)
            r[which] = (h[which].astype(f32) + l[which].astype(f32)) - approx
            item += 1


NEAR = 4


def chunks_of(part, replicas):
    unit = 8 * replicas
    units = part // unit
    lead = units - (2 * units) // 5
    pieces = [(0, lead * unit, True)]
    if units > lead:
        pieces.append((lead * unit, part - lead * unit, False))
    return pieces


def sum_kernel(replicas, over_tp, gather_tp, pieces, x, out, acc, in_tp, *rest):
    landing, (sems_s, sems_r) = rest[:-2], rest[-2:]
    near = NEAR
    far = replicas // near
    rep, tp = lax.axis_index("rep"), lax.axis_index("tp")
    a, b = lax.rem(rep, near), rep // near
    other = {"tp": 1 - tp, "rep": rep}

    def near_id(j):
        return {"rep": b * near + lax.rem(a + j, near), "tp": tp}

    def far_id(j):
        return {"rep": lax.rem(b + j, far) * near + a, "tp": tp}

    barrier = pltpu.get_barrier_semaphore()
    partners = [near_id(j) for j in range(1, near)] + [far_id(j) for j in range(1, far)]
    if over_tp or gather_tp:
        partners.append(other)
    for partner in partners:
        pl.semaphore_signal(barrier, inc=1, device_id=partner, device_id_type=MESH)
    pl.semaphore_wait(barrier, len(partners))

    counter = [0]

    def send(src, dst, device):
        i = counter[0]
        counter[0] += 1
        copy = pltpu.make_async_remote_copy(
            src_ref=src, dst_ref=dst, send_sem=sems_s.at[i], recv_sem=sems_r.at[i],
            device_id=device, device_id_type=MESH,
        )
        copy.start()
        return copy

    def finish(copies):
        for copy in copies:
            copy.wait()

    def ds(at, size):
        return pl.ds(pl.multiple_of(at, 8), size)

    rows = x.shape[0]
    part = rows // 2 if over_tp else rows
    base = tp * part if over_tp else 0
    shift = tp * rows if gather_tp else 0
    src = acc if over_tp else x
    levels = [(near, a, near_id), (far, b, far_id)]
    order = [levels if near_first else levels[::-1] for _, _, near_first in pieces]
    count = len(pieces)
    pending = [[] for _ in pieces]

    def scatter(k, ref, at, size, level):
        groups, me, ids = order[k][level]
        share = size // groups
        pending[k] = [
            send(
                ref.at[ds(at + lax.rem(me + j, groups) * share, share)],
                landing[2 * k + level].at[j - 1],
                ids(j),
            )
            for j in range(1, groups)
        ]

    def gather(k, at, size, devices):
        view = out.at[ds(shift + at, size)]
        pending[k] = [send(view, view, device) for device in devices]

    def reduced(k, ref, at, size, level):
        groups, me, _ = order[k][level]
        share = size // groups
        mine = at + me * share
        value = ref[ds(mine, share), :]
        for j in range(1, groups):
            value = value + landing[2 * k + level][j - 1]
        return mine, share, value

    if over_tp:
        for k, (start, size, _) in enumerate(pieces):
            theirs = x.at[ds((1 - tp) * part + start, size)]
            pending[k] = [send(theirs, in_tp.at[pl.ds(start, size)], other)]
    for k, (start, size, _) in enumerate(pieces):
        if over_tp:
            finish(pending[k])
            acc[ds(base + start, size), :] = (
                x[ds(base + start, size), :] + in_tp[pl.ds(start, size), :]
            )
        scatter(k, src, base + start, size, 0)
    held = []
    for k, (start, size, _) in enumerate(pieces):
        finish(pending[k])
        mine, share, value = reduced(k, src, base + start, size, 0)
        acc[ds(mine, share), :] = value
        held.append((mine, share))
        scatter(k, acc, mine, share, 1)
    for k in range(count):
        finish(pending[k])
        leaf, share, value = reduced(k, acc, held[k][0], held[k][1], 1)
        out[ds(shift + leaf, share), :] = value
        groups, _, ids = order[k][1]
        gather(k, leaf, share, [ids(j) for j in range(1, groups)])
    for k in range(count):
        finish(pending[k])
        groups, _, ids = order[k][0]
        gather(k, held[k][0], held[k][1], [ids(j) for j in range(1, groups)])
    for k, (start, size, _) in enumerate(pieces):
        finish(pending[k])
        pending[k] = []
        if over_tp or gather_tp:
            gather(k, base + start, size, [other])
    for k in range(count):
        finish(pending[k])


def all_sum(x, replicas, over_tp, gather_tp, collective_id):
    rows = x.shape[0]
    far = replicas // NEAR
    part = rows // 2 if over_tp else rows
    pieces = chunks_of(part, replicas)
    copies = 2 * (NEAR - 1 + far - 1 + 1) * len(pieces)
    landing = []
    for _, size, near_first in pieces:
        for groups in (NEAR, far) if near_first else (far, NEAR):
            size = size // groups
            landing.append(pltpu.VMEM((groups - 1, size, LANES), f32))
    return pl.pallas_call(
        functools.partial(sum_kernel, replicas, over_tp, gather_tp, pieces),
        out_shape=jax.ShapeDtypeStruct((rows * (2 if gather_tp else 1), LANES), f32),
        in_specs=[pl.BlockSpec(memory_space=pltpu.VMEM)],
        out_specs=pl.BlockSpec(memory_space=pltpu.VMEM),
        scratch_shapes=[pltpu.VMEM((rows, LANES), f32), pltpu.VMEM((part, LANES), f32)]
        + landing
        + [pltpu.SemaphoreType.DMA((copies,)), pltpu.SemaphoreType.DMA((copies,))],
        compiler_params=pltpu.CompilerParams(
            collective_id=collective_id, has_side_effects=True, vmem_limit_bytes=VMEM_LIMIT
        ),
        name=f"all_sum_{collective_id}",
    )(x)


def padded_sum(x, replicas, over_tp, gather_tp, collective_id):
    rows = x.shape[0]
    unit = 8 * replicas * (2 if over_tp else 1)
    extra = -rows % unit
    if extra:
        x = jnp.pad(x, ((0, extra), (0, 0)))
    total = all_sum(x, replicas, over_tp, gather_tp, collective_id)
    if extra:
        if gather_tp:
            total = total.reshape(2, rows + extra, LANES)[:, :rows].reshape(2 * rows, LANES)
        else:
            total = total[:rows]
    return total


def on_device(gn, en, sn, mn, gs, es, ss, ms):
    replicas = lax.axis_size("rep")
    shape_gn, shape_gs, shape_sn, shape_ss = gn.shape, gs.shape, sn.shape, ss.shape
    shape_mn, shape_ms = mn.shape, ms.shape
    gn, en, gs, es = (
        x.reshape((x.shape[1] * x.shape[2],) + x.shape[3:]) for x in (gn, en, gs, es)
    )
    sn, ss = (jnp.swapaxes(x.reshape((-1,) + x.shape[2:]), 1, 2) for x in (sn, ss))
    cn, depth, wn = gn.shape
    cs, _, ws = gs.shape
    rank = sn.shape[1]
    items = cn + cs
    steps, per, blocks = depth // BAND, BAND // LANES, depth // LANES
    factor_rows = (cn * wn + cs * ws) // LANES * rank
    mn = jnp.swapaxes(mn.reshape(cn, -1, LANES), 0, 1).reshape(-1, LANES)
    ms = ms.reshape(-1, LANES)

    band_n = pl.BlockSpec((cn, BAND, wn), lambda t: (0, t, 0))
    band_s = pl.BlockSpec((cs, BAND, ws), lambda t: (0, t, 0))
    bands = [band_n, band_n, band_s, band_s]

    def full(shape):
        return pl.BlockSpec(shape, lambda t: (0,) * len(shape))

    panel_band = pl.BlockSpec((per, items * rank, LANES), lambda t: (t, 0, 0))
    panel_shape = jax.ShapeDtypeStruct((blocks, items * rank, LANES), f32)
    keep = [pltpu.VMEM((cn, 2 * rank, wn), bf16), pltpu.VMEM((cs, 2 * rank, ws), bf16)]
    params = pltpu.CompilerParams(vmem_limit_bytes=VMEM_LIMIT)

    panel, hn, ln, hs, ls = pl.pallas_call(
        functools.partial(first_left_kernel, rank),
        grid=(steps,),
        in_specs=bands + [full(sn.shape), full(ss.shape)],
        out_specs=[panel_band] + bands,
        out_shape=[
            panel_shape,
            jax.ShapeDtypeStruct(gn.shape, bf16),
            jax.ShapeDtypeStruct(gn.shape, bf16),
            jax.ShapeDtypeStruct(gs.shape, bf16),
            jax.ShapeDtypeStruct(gs.shape, bf16),
        ],
        scratch_shapes=keep,
        compiler_params=params,
        name="first_left",
    )(gn, en, gs, es, sn, ss)

    for turn in range(ROUNDS):
        if turn:
            panel = pl.pallas_call(
                functools.partial(left_kernel, rank, replicas),
                grid=(steps,),
                in_specs=[full(factor.shape)] + bands,
                out_specs=panel_band,
                out_shape=panel_shape,
                scratch_shapes=keep,
                compiler_params=params,
                name="left",
            )(factor, hn, ln, hs, ls)
        panel = padded_sum(panel.reshape(-1, LANES), replicas, True, False, 0)
        panel = panel.reshape(panel_shape.shape)
        ortho, factor = pl.pallas_call(
            functools.partial(right_kernel, rank, items),
            grid=(steps,),
            in_specs=[full(panel_shape.shape)] + bands,
            out_specs=[full(panel_shape.shape), full((factor_rows, LANES))],
            out_shape=[panel_shape, jax.ShapeDtypeStruct((factor_rows, LANES), f32)],
            compiler_params=params,
            name="right",
        )(panel, hn, ln, hs, ls)
        final = turn == ROUNDS - 1
        factor = padded_sum(factor, replicas, False, final, 2 if final else 1)

    rn, rs, fn, fs, vn, vs = pl.pallas_call(
        functools.partial(last_kernel, rank, replicas),
        grid=(steps,),
        in_specs=[full(panel_shape.shape), full(factor.shape)]
        + bands
        + [full(mn.shape), full(ms.shape)],
        out_specs=[
            band_n, band_s, full(sn.shape), full(ss.shape), full(mn.shape), full(ms.shape),
        ],
        out_shape=[
            jax.ShapeDtypeStruct(x.shape, f32) for x in (gn, gs, sn, ss, mn, ms)
        ],
        scratch_shapes=[
            pltpu.VMEM((cn, 3 * rank, wn), bf16),
            pltpu.VMEM((cs, 3 * rank, ws), bf16),
            pltpu.VMEM((2 * wn // LANES, LANES, LANES), f32),
            pltpu.VMEM((2 * ws // LANES, LANES, LANES), f32),
        ],
        compiler_params=params,
        name="last",
    )(ortho, factor, hn, ln, hs, ls, mn, ms)
    return (
        rn.reshape(shape_gn),
        jnp.swapaxes(fn, 1, 2).reshape(shape_sn),
        jnp.swapaxes(vn.reshape(-1, cn, LANES), 0, 1).reshape(shape_mn),
        rs.reshape(shape_gs),
        jnp.swapaxes(fs, 1, 2).reshape(shape_ss),
        vs.reshape(shape_ms),
    )


def solution(mesh):
    in_specs = (
        P("rep", None, None, None, "tp"),
        P("rep", None, None, None, "tp"),
        P(None, None, "tp", None),
        P(None, None, ("rep", "tp")),
        P("rep", None, None, None, "tp"),
        P("rep", None, None, None, "tp"),
        P(None, None, "tp", None),
        P(None, None, ("rep", "tp")),
    )
    out_specs = (
        P("rep", None, None, None, "tp"),
        P(None, None, "tp", None),
        P(None, None, ("rep", "tp")),
        P("rep", None, None, None, "tp"),
        P(None, None, "tp", None),
        P(None, None, ("rep", "tp")),
    )
    return jax.shard_map(
        on_device, mesh=mesh, in_specs=in_specs, out_specs=out_specs, check_vma=False
    )
```
